256 devices in a mesh: row: 32 (over x, y, core), feat: 8 (over z).
Axes of the slice: x: 4, y: 4, z: 8, core: 2. Of those that a mesh axis runs over, the one named last changes fastest.
Arguments:
- bins: int32 [1024, 262144], P('feat', 'row'), may hold values from 0 to 255
- grads: bfloat16 [262144], P('row'), may hold values from -6 to 6
- hess: bfloat16 [262144], P('row'), may hold values from 0.049804688 to 1
- node: int32 [262144], P('row'), may hold values from 0 to 7
Outputs:
- shortfall: float32 [1024, 8, 256], P(('feat', 'row'))
- best: float32 [8], replicated
The draws below stay inside these ranges and needn't reach their ends.
All inputs are finite; a program needn't handle non-finite values.
Results may differ from the reference program's by a relative error of at most 0.0003.
Values sent between devices are 32-bit elements; how exact they have to be, the bound alone decides.
No kernel may reach another device: no remote copies, remote signals or barrier semaphores. Data moves between devices by JAX's collectives and lax.ppermute only.
A program may use at most 64 MiB of HBM per device.

```python
import math
import jax
import jax.numpy as jnp
from jax import lax

FEATURES = 1024
BINS = 256
NODES = 8
ROWS = 262144


def plant(entries, key, smallest, largest):
    dims = entries.shape
    index_at = [jax.random.randint(jax.random.fold_in(key, axis), (), 0, dims[axis]) for axis in range(len(dims))]
    entries = entries.at[tuple(index_at)].set(smallest)
    longest = dims.index(max(dims))
    index_at[longest] = (index_at[longest] + 1) % dims[longest]
    return entries.at[tuple(index_at)].set(largest)


def block_levels(rng, shape, cuts, least, high):
    def one(axis_at, parts):
        steps = jax.random.uniform(jax.random.fold_in(jax.random.fold_in(rng, 6), axis_at), (parts,), jnp.float32, least / len(cuts), high / len(cuts))
        return jnp.repeat(jnp.exp(steps), shape[axis_at] // parts).reshape((-1,) + (1,) * (len(shape) - axis_at - 1))

    level = one(*cuts[0])
    for cut in cuts[1:]:
        level = level * one(*cut)
    return level


def scatter_about(stream_key, dims, spread, reach, split=(), held_as=jnp.bfloat16):
    loudness = block_levels(stream_key, dims, split, -0.22, 0.18) if split else 1.0
    result = jax.random.normal(stream_key, dims, jnp.float32) * spread * loudness
    return jnp.minimum(jnp.maximum(result, -reach), reach).astype(held_as)


def setup_inputs(seed: int = 0) -> dict:
    key_of = jax.random.split(jax.random.key(seed), 5)
    bins = plant(jax.random.randint(key_of[0], (FEATURES, ROWS), 0, BINS), jax.random.fold_in(key_of[0], 1), 0, BINS - 1).astype(jnp.int32)
    grads = scatter_about(key_of[1], (ROWS,), 1.0, 6.0, ((0, 32),))
    hess = jnp.clip(jnp.exp(math.log(1.0) - 2.9996462 * jax.random.uniform(key_of[2], (ROWS,), jnp.float32) ** block_levels(key_of[2], (ROWS,), ((0, 32),), -0.2, 0.2)), 0.049804688, 1.0).astype(jnp.bfloat16)
    node = plant(jax.random.randint(key_of[3], (ROWS,), 0, NODES), jax.random.fold_in(key_of[3], 1), 0, NODES - 1).astype(jnp.int32)
    return dict(bins=bins, grads=grads, hess=hess, node=node)


def reference(bins, grads, hess, node):
    stats = jnp.stack([grads.astype(jnp.float32), hess.astype(jnp.float32)], axis=1)

    def one_feature(column):
        labels = (node * BINS + column).astype(jnp.int32)
        summed = jax.ops.segment_sum(stats, labels, num_segments=NODES * BINS)
        return jnp.transpose(summed.reshape(NODES, BINS, 2), (2, 0, 1))

    hist = lax.map(one_feature, bins)
    totals = jax.ops.segment_sum(stats, node.astype(jnp.int32), num_segments=NODES)
    left = jnp.cumsum(hist, axis=3)
    grad_left = left[:, 0]
    hess_left = left[:, 1]
    grad_total = totals[:, 0][None, :, None]
    hess_total = totals[:, 1][None, :, None]
    gain = grad_left * grad_left / (hess_left + 1.0)
    gain = gain + (grad_total - grad_left) ** 2 / (hess_total - hess_left + 1.0)
    gain = gain - grad_total * grad_total / (hess_total + 1.0)
    best = jnp.max(gain, axis=(0, 2))
    return gain - best[None, :, None], best
```

```python
import functools

import jax
import jax.numpy as jnp
from jax import lax
from jax.experimental import pallas as pl
from jax.experimental.pallas import tpu as pltpu
from jax.sharding import PartitionSpec as P

BINS = 256
NODES = 8
STATS = 2 * NODES
LOW = 64
HIGH = BINS // LOW
GROUP = BINS // LOW
SUB = 8
CHUNK = 512


def hist_kernel(bins_ref, weighted_ref, out_ref):
    rows = bins_ref.shape[1]
    level = lax.broadcasted_iota(jnp.int32, (STATS, CHUNK), 0)
    zero = jnp.zeros((), jnp.bfloat16)
    one = jnp.ones((), jnp.bfloat16)
    for group in range(SUB // GROUP):
        total = jnp.zeros((GROUP * HIGH * STATS, GROUP * LOW), jnp.float32)
        for chunk in range(rows // CHUNK):
            at = slice(chunk * CHUNK, (chunk + 1) * CHUNK)
            columns = bins_ref[group * GROUP : (group + 1) * GROUP, at]
            weighted = weighted_ref[:, at]
            low = columns & (LOW - 1)
            high = columns >> (LOW.bit_length() - 1)
            left = []
            right = []
            for j in range(GROUP):
                low_j = jnp.broadcast_to(low[j : j + 1].astype(jnp.bfloat16), (STATS, CHUNK))
                for i in range(LOW // STATS):
                    wanted = (level + STATS * i).astype(jnp.bfloat16)
                    right.append(jnp.where(low_j == wanted, one, zero))
                high_j = jnp.broadcast_to(high[j : j + 1].astype(jnp.bfloat16), (STATS, CHUNK))
                for q in range(HIGH):
                    left.append(jnp.where(high_j == jnp.asarray(q, jnp.bfloat16), weighted, zero))
            total = total + lax.dot_general(
                jnp.concatenate(left, 0),
                jnp.concatenate(right, 0),
                (((1,), (1,)), ((), ())),
                preferred_element_type=jnp.float32,
            )
        for j in range(GROUP):
            blocks = [
                total[(j * HIGH + q) * STATS : (j * HIGH + q + 1) * STATS, j * LOW : (j + 1) * LOW]
                for q in range(HIGH)
            ]
            out_ref[group * GROUP + j] = jnp.concatenate(blocks, axis=1)


def histogram(bins, weighted):
    features, rows = bins.shape
    return pl.pallas_call(
        hist_kernel,
        grid=(features // SUB,),
        in_specs=[pl.BlockSpec((SUB, rows), lambda i: (i, 0)), pl.BlockSpec((STATS, rows), lambda i: (0, 0))],
        out_specs=pl.BlockSpec((SUB, STATS, BINS), lambda i: (i, 0, 0)),
        out_shape=jax.ShapeDtypeStruct((features, STATS, BINS), jnp.float32),
        compiler_params=pltpu.CompilerParams(vmem_limit_bytes=48 * 2**20),
        cost_estimate=pl.CostEstimate(
            flops=2 * features * rows * STATS * BINS, bytes_accessed=4 * features * rows, transcendentals=0
        ),
        name="histogram",
    )(bins, weighted)


def gain_kernel(parts_ref, gain_ref, best_ref):
    count = parts_ref.shape[0]
    hist = parts_ref[0]
    for i in range(1, count):
        hist = hist + parts_ref[i]
    upper = lax.broadcasted_iota(jnp.int32, (BINS, BINS), 0) <= lax.broadcasted_iota(jnp.int32, (BINS, BINS), 1)
    left = lax.dot_general(
        hist,
        upper.astype(jnp.float32),
        (((1,), (0,)), ((), ())),
        precision=lax.Precision.HIGHEST,
        preferred_element_type=jnp.float32,
    )
    best = None
    for f in range(gain_ref.shape[0]):
        grad_left = left[f * STATS : f * STATS + NODES]
        hess_left = left[f * STATS + NODES : (f + 1) * STATS]
        grad_total = grad_left[:, BINS - 1 :]
        hess_total = hess_left[:, BINS - 1 :]
        gain = grad_left * grad_left / (hess_left + 1.0)
        gain = gain + (grad_total - grad_left) ** 2 / (hess_total - hess_left + 1.0)
        gain = gain - grad_total * grad_total / (hess_total + 1.0)
        gain_ref[f] = gain
        most = jnp.max(gain, axis=1, keepdims=True)
        best = most if best is None else jnp.maximum(best, most)
    best_ref[...] = jnp.broadcast_to(best, best_ref.shape)


def gains(parts):
    share = parts.shape[1]
    count = parts.shape[0]
    return pl.pallas_call(
        gain_kernel,
        out_shape=(
            jax.ShapeDtypeStruct((share, NODES, BINS), jnp.float32),
            jax.ShapeDtypeStruct((NODES, 128), jnp.float32),
        ),
        compiler_params=pltpu.CompilerParams(vmem_limit_bytes=48 * 2**20),
        name="gains",
    )(parts.reshape(count, share * STATS, BINS))


def per_device(bins, grads, hess, node):
    features = bins.shape[0]
    row_size = lax.axis_size("row")
    device_count = row_size * lax.axis_size("feat")
    share = features // row_size
    member = node[None, :] == jnp.arange(NODES, dtype=jnp.int32)[:, None]
    zero = jnp.zeros((), jnp.bfloat16)
    weighted = jnp.concatenate(
        [jnp.where(member, grads[None, :], zero), jnp.where(member, hess[None, :], zero)], axis=0
    )
    partial_hist = histogram(bins, weighted)
    parts = lax.all_to_all(partial_hist.reshape(row_size, share, STATS, BINS), "row", 0, 0)
    gain, own_best = gains(parts)
    copies = jnp.broadcast_to(own_best[None, :, 0], (device_count, NODES))
    best = jnp.max(lax.all_to_all(copies, ("row", "feat"), 0, 0), axis=0)
    return (gain - best[None, :, None], best)


def solution(mesh):
    return jax.shard_map(
        per_device,
        mesh=mesh,
        in_specs=(P("feat", "row"), P("row"), P("row"), P("row")),
        out_specs=(P(("feat", "row"), None, None), P()),
        check_vma=False,
    )
```

```python
import functools

import jax
import jax.numpy as jnp
from jax import lax
from jax.experimental import pallas as pl
from jax.experimental.pallas import tpu as pltpu
from jax.sharding import PartitionSpec as P

BINS = 256
NODES = 8
STATS = 2 * NODES
LOW = 64
HIGH = BINS // LOW
GROUP = BINS // LOW
SUB = 16
CHUNK = 512
SHARE = 4
CORES = 2
PIECES = ((0, 1), (2, 3))


def hist_kernel(picks, core_ref, bins_ref, weighted_ref, keep_ref, send_ref, held_ref):
    rows = bins_ref.shape[1]
    core = core_ref[0]
    level = lax.broadcasted_iota(jnp.int32, (STATS, CHUNK), 0)
    zero = jnp.zeros((), jnp.bfloat16)
    one = jnp.ones((), jnp.bfloat16)
    features = [(owner, slot) for owner in range(SUB // SHARE) for slot in range(len(picks))]
    for first in range(0, len(features), GROUP):
        group = features[first : first + GROUP]
        total = jnp.zeros((GROUP * HIGH * STATS, GROUP * LOW), jnp.float32)
        for chunk in range(rows // CHUNK):
            at = slice(chunk * CHUNK, (chunk + 1) * CHUNK)
            weighted = weighted_ref[:, at]
            left = []
            right = []
            for owner, slot in group:
                column = bins_ref[owner * SHARE + picks[slot] : owner * SHARE + picks[slot] + 1, at]
                low = (column & (LOW - 1)).astype(jnp.bfloat16)
                high = (column >> (LOW.bit_length() - 1)).astype(jnp.bfloat16)
                low = jnp.broadcast_to(low, (STATS, CHUNK))
                for i in range(LOW // STATS):
                    wanted = (level + STATS * i).astype(jnp.bfloat16)
                    right.append(jnp.where(low == wanted, one, zero))
                high = jnp.broadcast_to(high, (STATS, CHUNK))
                for q in range(HIGH):
                    left.append(jnp.where(high == jnp.asarray(q, jnp.bfloat16), weighted, zero))
            total = total + lax.dot_general(
                jnp.concatenate(left, 0),
                jnp.concatenate(right, 0),
                (((1,), (1,)), ((), ())),
                preferred_element_type=jnp.float32,
            )
        for j, (owner, slot) in enumerate(group):
            blocks = [
                total[(j * HIGH + q) * STATS : (j * HIGH + q + 1) * STATS, j * LOW : (j + 1) * LOW]
                for q in range(HIGH)
            ]
            held_ref[owner, slot] = jnp.concatenate(blocks, axis=1)
    for chip in range(SUB // SHARE // CORES):
        first, second = held_ref[chip * CORES], held_ref[chip * CORES + 1]
        keep_ref[chip] = jnp.where(core == 0, first, second)
        send_ref[chip] = jnp.where(core == 0, second, first)


def histogram(bins, weighted, core, picks):
    features, rows = bins.shape
    chips = features // (SHARE * CORES)
    step = SUB // (SHARE * CORES)
    count = len(picks)
    return pl.pallas_call(
        functools.partial(hist_kernel, picks),
        grid=(features // SUB,),
        in_specs=[
            pl.BlockSpec(memory_space=pltpu.SMEM),
            pl.BlockSpec((SUB, rows), lambda i: (i, 0)),
            pl.BlockSpec((STATS, rows), lambda i: (0, 0)),
        ],
        out_specs=[pl.BlockSpec((step, count, STATS, BINS), lambda i: (i, 0, 0, 0))] * 2,
        out_shape=[jax.ShapeDtypeStruct((chips, count, STATS, BINS), jnp.float32)] * 2,
        scratch_shapes=[pltpu.VMEM((SUB // SHARE, count, STATS, BINS), jnp.float32)],
        compiler_params=pltpu.CompilerParams(vmem_limit_bytes=60 * 2**20),
        cost_estimate=pl.CostEstimate(
            flops=2 * features * count // SHARE * rows * LOW * BINS,
            bytes_accessed=4 * features * rows,
            transcendentals=0,
        ),
        name="histogram",
    )(core, bins, weighted)


def gain_kernel(*refs):
    parts, (gain_ref, best_ref) = refs[: len(PIECES)], refs[len(PIECES) :]
    upper = lax.broadcasted_iota(jnp.int32, (BINS, BINS), 0) <= lax.broadcasted_iota(jnp.int32, (BINS, BINS), 1)
    upper = upper.astype(jnp.float32)
    best = None
    for picks, ref in zip(PIECES, parts):
        hist = ref[0]
        for i in range(1, ref.shape[0]):
            hist = hist + ref[i]
        left = lax.dot_general(
            hist,
            upper,
            (((1,), (0,)), ((), ())),
            precision=lax.Precision.HIGHEST,
            preferred_element_type=jnp.float32,
        )
        for slot, feature in enumerate(picks):
            grad_left = left[slot * STATS : slot * STATS + NODES]
            hess_left = left[slot * STATS + NODES : (slot + 1) * STATS]
            grad_total = grad_left[:, BINS - 1 :]
            hess_total = hess_left[:, BINS - 1 :]
            gain = grad_left * grad_left / (hess_left + 1.0)
            gain = gain + (grad_total - grad_left) ** 2 / (hess_total - hess_left + 1.0)
            gain = gain - grad_total * grad_total / (hess_total + 1.0)
            gain_ref[feature] = gain
            most = jnp.max(gain, axis=1, keepdims=True)
            best = most if best is None else jnp.maximum(best, most)
    best_ref[...] = jnp.broadcast_to(best, best_ref.shape)


def gains(*parts):
    parts = [p.reshape(p.shape[0], p.shape[1] * STATS, BINS) for p in parts]
    return pl.pallas_call(
        gain_kernel,
        out_shape=(
            jax.ShapeDtypeStruct((SHARE, NODES, BINS), jnp.float32),
            jax.ShapeDtypeStruct((NODES, 128), jnp.float32),
        ),
        compiler_params=pltpu.CompilerParams(vmem_limit_bytes=60 * 2**20),
        name="gains",
    )(*parts)


def per_device(bins, grads, hess, node):
    row_size = lax.axis_size("row")
    feat_size = lax.axis_size("feat")
    chips = row_size // CORES
    swap = [(i, i ^ 1) for i in range(row_size)]
    same_core = [[chip * CORES + c for chip in range(chips)] for c in range(CORES)]
    same_core_all = [[i * feat_size + z for i in group for z in range(feat_size)] for group in same_core]
    member = node[None, :] == jnp.arange(NODES, dtype=jnp.int32)[:, None]
    zero = jnp.zeros((), jnp.bfloat16)
    weighted = jnp.concatenate(
        [jnp.where(member, grads[None, :], zero), jnp.where(member, hess[None, :], zero)], axis=0
    )
    core = (lax.axis_index("row") % CORES)[None]
    parts = []
    for picks in PIECES:
        keep, send = histogram(bins, weighted, core, picks)
        if parts:
            send, parts[-1] = lax.optimization_barrier((send, parts[-1]))
        pair = keep + lax.ppermute(send, "row", swap)
        pair, weighted = lax.optimization_barrier((pair, weighted))
        parts.append(lax.all_to_all(pair, "row", 0, 0, axis_index_groups=same_core, tiled=True))
    gain, own_best = gains(*parts)
    own_best = own_best[:, 0]
    own_best = jnp.maximum(own_best, lax.ppermute(own_best, "row", swap))
    copies = jnp.broadcast_to(own_best, (chips * feat_size, NODES))
    best = jnp.max(lax.all_to_all(copies, ("row", "feat"), 0, 0, axis_index_groups=same_core_all, tiled=True), axis=0)
    return (gain - best[None, :, None], best)


def solution(mesh):
    return jax.shard_map(
        per_device,
        mesh=mesh,
        in_specs=(P("feat", "row"), P("row"), P("row"), P("row")),
        out_specs=(P(("feat", "row"), None, None), P()),
        check_vma=False,
    )
```

```python
import functools

import jax
import jax.numpy as jnp
from jax import lax
from jax.experimental import pallas as pl
from jax.experimental.pallas import tpu as pltpu
from jax.sharding import PartitionSpec as P

BINS = 256
NODES = 8
STATS = 2 * NODES
LOW = 64
HIGH = BINS // LOW
GROUP = BINS // LOW
SUB = 16
CHUNK = 512
SHARE = 4
CORES = 2
PIECES = ((0, 1, 2, 3),)


def hist_kernel(picks, core_ref, bins_ref, weighted_ref, keep_ref, send_ref, held_ref):
    rows = bins_ref.shape[1]
    core = core_ref[0]
    level = lax.broadcasted_iota(jnp.int32, (STATS, CHUNK), 0)
    zero = jnp.zeros((), jnp.bfloat16)
    one = jnp.ones((), jnp.bfloat16)
    features = [(owner, slot) for owner in range(SUB // SHARE) for slot in range(len(picks))]
    for first in range(0, len(features), GROUP):
        group = features[first : first + GROUP]
        total = jnp.zeros((GROUP * HIGH * STATS, GROUP * LOW), jnp.float32)
        for chunk in range(rows // CHUNK):
            at = slice(chunk * CHUNK, (chunk + 1) * CHUNK)
            weighted = weighted_ref[:, at]
            left = []
            right = []
            for owner, slot in group:
                column = bins_ref[owner * SHARE + picks[slot] : owner * SHARE + picks[slot] + 1, at]
                low = (column & (LOW - 1)).astype(jnp.bfloat16)
                high = (column >> (LOW.bit_length() - 1)).astype(jnp.bfloat16)
                low = jnp.broadcast_to(low, (STATS, CHUNK))
                for i in range(LOW // STATS):
                    wanted = (level + STATS * i).astype(jnp.bfloat16)
                    right.append(jnp.where(low == wanted, one, zero))
                high = jnp.broadcast_to(high, (STATS, CHUNK))
                for q in range(HIGH):
                    left.append(jnp.where(high == jnp.asarray(q, jnp.bfloat16), weighted, zero))
            total = total + lax.dot_general(
                jnp.concatenate(left, 0),
                jnp.concatenate(right, 0),
                (((1,), (1,)), ((), ())),
                preferred_element_type=jnp.float32,
            )
        for j, (owner, slot) in enumerate(group):
            blocks = [
                total[(j * HIGH + q) * STATS : (j * HIGH + q + 1) * STATS, j * LOW : (j + 1) * LOW]
                for q in range(HIGH)
            ]
            held_ref[owner, slot] = jnp.concatenate(blocks, axis=1)
    for chip in range(SUB // SHARE // CORES):
        first, second = held_ref[chip * CORES], held_ref[chip * CORES + 1]
        keep_ref[chip] = jnp.where(core == 0, first, second)
        send_ref[chip] = jnp.where(core == 0, second, first)


def histogram(bins, weighted, core, picks):
    features, rows = bins.shape
    chips = features // (SHARE * CORES)
    step = SUB // (SHARE * CORES)
    count = len(picks)
    return pl.pallas_call(
        functools.partial(hist_kernel, picks),
        grid=(features // SUB,),
        in_specs=[
            pl.BlockSpec(memory_space=pltpu.SMEM),
            pl.BlockSpec((SUB, rows), lambda i: (i, 0)),
            pl.BlockSpec((STATS, rows), lambda i: (0, 0)),
        ],
        out_specs=[pl.BlockSpec((step, count, STATS, BINS), lambda i: (i, 0, 0, 0))] * 2,
        out_shape=[jax.ShapeDtypeStruct((chips, count, STATS, BINS), jnp.float32)] * 2,
        scratch_shapes=[pltpu.VMEM((SUB // SHARE, count, STATS, BINS), jnp.float32)],
        compiler_params=pltpu.CompilerParams(vmem_limit_bytes=48 * 2**20),
        cost_estimate=pl.CostEstimate(
            flops=2 * features * count // SHARE * rows * LOW * BINS,
            bytes_accessed=4 * features * rows,
            transcendentals=0,
        ),
        name="histogram",
    )(core, bins, weighted)


def gain_kernel(*refs):
    parts, (gain_ref, best_ref) = refs[: len(PIECES)], refs[len(PIECES) :]
    upper = lax.broadcasted_iota(jnp.int32, (BINS, BINS), 0) <= lax.broadcasted_iota(jnp.int32, (BINS, BINS), 1)
    upper = upper.astype(jnp.float32)
    best = None
    for picks, ref in zip(PIECES, parts):
        hist = ref[0]
        for i in range(1, ref.shape[0]):
            hist = hist + ref[i]
        left = lax.dot_general(
            hist,
            upper,
            (((1,), (0,)), ((), ())),
            precision=lax.Precision.HIGHEST,
            preferred_element_type=jnp.float32,
        )
        for slot, feature in enumerate(picks):
            grad_left = left[slot * STATS : slot * STATS + NODES]
            hess_left = left[slot * STATS + NODES : (slot + 1) * STATS]
            grad_total = grad_left[:, BINS - 1 :]
            hess_total = hess_left[:, BINS - 1 :]
            gain = grad_left * grad_left / (hess_left + 1.0)
            gain = gain + (grad_total - grad_left) ** 2 / (hess_total - hess_left + 1.0)
            gain = gain - grad_total * grad_total / (hess_total + 1.0)
            gain_ref[feature] = gain
            most = jnp.max(gain, axis=1, keepdims=True)
            best = most if best is None else jnp.maximum(best, most)
    best_ref[...] = jnp.broadcast_to(best, best_ref.shape)


def gains(*parts):
    parts = [p.reshape(p.shape[0], p.shape[1] * STATS, BINS) for p in parts]
    return pl.pallas_call(
        gain_kernel,
        out_shape=(
            jax.ShapeDtypeStruct((SHARE, NODES, BINS), jnp.float32),
            jax.ShapeDtypeStruct((NODES, 128), jnp.float32),
        ),
        compiler_params=pltpu.CompilerParams(vmem_limit_bytes=48 * 2**20),
        name="gains",
    )(*parts)


def per_device(bins, grads, hess, node):
    row_size = lax.axis_size("row")
    feat_size = lax.axis_size("feat")
    chips = row_size // CORES
    swap = [(i, i ^ 1) for i in range(row_size)]
    same_core = [[chip * CORES + c for chip in range(chips)] for c in range(CORES)]
    member = node[None, :] == jnp.arange(NODES, dtype=jnp.int32)[:, None]
    zero = jnp.zeros((), jnp.bfloat16)
    weighted = jnp.concatenate(
        [jnp.where(member, grads[None, :], zero), jnp.where(member, hess[None, :], zero)], axis=0
    )
    core = (lax.axis_index("row") % CORES)[None]
    parts = []
    for picks in PIECES:
        keep, send = histogram(bins, weighted, core, picks)
        pair = keep + lax.ppermute(send, "row", swap)
        parts.append(lax.all_to_all(pair, "row", 0, 0, axis_index_groups=same_core, tiled=True))
    gain, own_best = gains(*parts)
    own_best = own_best[:, 0]
    copies = jnp.broadcast_to(own_best, (row_size * feat_size, NODES))
    best = jnp.max(lax.all_to_all(copies, ("row", "feat"), 0, 0, tiled=True), axis=0)
    return (gain - best[None, :, None], best)


def solution(mesh):
    return jax.shard_map(
        per_device,
        mesh=mesh,
        in_specs=(P("feat", "row"), P("row"), P("row"), P("row")),
        out_specs=(P(("feat", "row"), None, None), P()),
        check_vma=False,
    )
```

```python
import functools

import jax
import jax.numpy as jnp
from jax import lax
from jax.experimental import pallas as pl
from jax.experimental.pallas import tpu as pltpu
from jax.sharding import PartitionSpec as P

BINS = 256
NODES = 8
LANES = 128
CHUNK = 256
LOW = 16
HIGH = BINS // LOW
CORES = 2
SHARE = 4
BYTES = 4
TILES = 16
BOTH = 2 * HIGH


def iota(shape, dim):
    return lax.broadcasted_iota(jnp.int32, shape, dim)


def ones_where(condition, dtype=jnp.float32):
    return jnp.where(condition, 1.0, 0.0).astype(dtype)


def exact_dot(a, b):
    return jnp.dot(a, b, preferred_element_type=jnp.float32, precision=lax.Precision.HIGHEST)


def dot_t(a, b):
    return lax.dot_general(a, b, (((1,), (1,)), ((), ())), preferred_element_type=jnp.float32)


def plan_kernel(node_ref, table_ref, order_ref):
    tiles = node_ref.shape[0]
    node = node_ref[...]
    members = [node == n for n in range(NODES)]
    stacked = jnp.concatenate([ones_where(m) for m in members], 0).astype(jnp.bfloat16)
    before = ones_where(iota((LANES, LANES), 0) < iota((LANES, LANES), 1), jnp.bfloat16)
    ranks = jnp.dot(stacked, before, preferred_element_type=jnp.float32)
    place = jnp.zeros((tiles, LANES), jnp.float32)
    first = jnp.zeros((tiles, 1), jnp.float32)
    counts = jnp.zeros((NODES, tiles), jnp.float32)
    for n in range(NODES):
        at = slice(n * tiles, (n + 1) * tiles)
        place = place + jnp.where(members[n], ranks[at] + first, 0.0)
        first = first + jnp.sum(ones_where(members[n]), axis=1, keepdims=True)
        counts = counts + dot_t(ones_where(iota((NODES, LANES), 0) == n, jnp.bfloat16), stacked[at])
    earlier = exact_dot(counts, ones_where(iota((tiles, tiles), 0) < iota((tiles, tiles), 1)))
    lower = ones_where(iota((NODES, NODES), 0) > iota((NODES, NODES), 1))
    start = exact_dot(lower, counts)
    total = jnp.sum(counts, axis=1, keepdims=True).astype(jnp.int32)
    padded = ((total + (CHUNK - 1)) // CHUNK * CHUNK).astype(jnp.float32)
    base = exact_dot(lower, jnp.broadcast_to(padded, (NODES, LANES)))
    ended = ones_where(base + padded <= (iota((NODES, LANES), 1) * CHUNK).astype(jnp.float32))
    owner = jnp.minimum(jnp.sum(ended, axis=0, keepdims=True), NODES - 1.0)
    table_ref[0:NODES, :tiles] = (base[:, :tiles] + earlier).astype(jnp.int32)
    table_ref[NODES : 2 * NODES, :tiles] = counts.astype(jnp.int32)
    table_ref[2 * NODES : 3 * NODES, :tiles] = start.astype(jnp.int32)
    table_ref[3 * NODES : 4 * NODES, :] = jnp.broadcast_to(owner, (NODES, LANES)).astype(jnp.int32)
    lane = iota((8, LANES), 1).astype(jnp.bfloat16)
    slot = iota((LANES, LANES), 0).astype(jnp.float32)
    for t in range(tiles):
        hit = ones_where(jnp.broadcast_to(place[t : t + 1], (LANES, LANES)) == slot, jnp.bfloat16)
        order_ref[t] = dot_t(lane, hit).astype(jnp.int32)


def plan(node):
    tiles = node.shape[0] // LANES
    return pl.pallas_call(
        plan_kernel,
        out_shape=(
            jax.ShapeDtypeStruct((4 * NODES, LANES), jnp.int32),
            jax.ShapeDtypeStruct((tiles, 8, LANES), jnp.int32),
        ),
        compiler_params=pltpu.CompilerParams(vmem_limit_bytes=16 * 2**20),
        name="plan",
    )(node.reshape(tiles, LANES))


def place_kernel(table_ref, bins_ref, grads_ref, hess_ref, order_ref, packed_ref, stats_ref):
    step = pl.program_id(0)

    @pl.when(step == 0)
    def _():
        stats_ref[...] = jnp.zeros_like(stats_ref)

    lane = iota((8, LANES), 1)
    top = iota((8, LANES), 0) == 0
    groups = packed_ref.shape[1] // 8
    for i in range(TILES):
        at = slice(i * LANES, (i + 1) * LANES)
        t = step * TILES + i
        values = []
        for g in range(groups):
            word = bins_ref[8 * g : 8 * g + 8, at]
            for k in range(1, BYTES):
                first = 8 * (g + groups * k)
                word = word | (bins_ref[first : first + 8, at] << (8 * k))
            values.append(word)
        grad = jnp.broadcast_to(grads_ref[:, at].astype(jnp.float32), (8, LANES))
        hess = jnp.broadcast_to(hess_ref[:, at].astype(jnp.float32), (8, LANES))
        values.append(jnp.where(top, grad, hess))
        order = order_ref[i]
        values = [jnp.take_along_axis(v, order, axis=1) for v in values]
        for n in range(NODES):
            dest = table_ref[n, t]
            count = table_ref[NODES + n, t]
            start = table_ref[2 * NODES + n, t]
            tile = dest >> 7
            off = dest & (LANES - 1)
            inside = ((lane - off) & (LANES - 1)) < count
            here = inside & (lane >= off)
            beyond = inside & (lane < off)
            for g, value in enumerate(values):
                moved = pltpu.roll(value, (off - start) & (LANES - 1), axis=1)
                ref, rows = (packed_ref, slice(8 * g, 8 * g + 8)) if g < groups else (stats_ref, slice(0, 8))
                pltpu.store(ref.at[tile, rows], moved, mask=here)
                pltpu.store(ref.at[tile + 1, rows], moved, mask=beyond)


def place(table, order, bins, grads, hess):
    features, rows = bins.shape
    tiles = rows // LANES
    room = tiles + 2 * NODES
    words = features // BYTES
    width = TILES * LANES
    return pl.pallas_call(
        place_kernel,
        grid=(tiles // TILES,),
        in_specs=[
            pl.BlockSpec(memory_space=pltpu.SMEM),
            pl.BlockSpec((features, width), lambda i: (0, i)),
            pl.BlockSpec((1, width), lambda i: (0, i)),
            pl.BlockSpec((1, width), lambda i: (0, i)),
            pl.BlockSpec((TILES, 8, LANES), lambda i: (i, 0, 0)),
        ],
        out_specs=[
            pl.BlockSpec((room, words, LANES), lambda i: (0, 0, 0)),
            pl.BlockSpec((room, 8, LANES), lambda i: (0, 0, 0)),
        ],
        out_shape=[
            jax.ShapeDtypeStruct((room, words, LANES), jnp.int32),
            jax.ShapeDtypeStruct((room, 8, LANES), jnp.float32),
        ],
        compiler_params=pltpu.CompilerParams(vmem_limit_bytes=50 * 2**20),
        name="place",
    )(table, bins, grads[None], hess[None], order)


def hist_kernel(chunks, per_step, core_ref, table_ref, packed_ref, stats_ref, keep_ref, send_ref, spread_ref, sums_ref):
    core = core_ref[0]
    level = iota((HIGH, CHUNK), 0).astype(jnp.bfloat16)
    zero = jnp.zeros((), jnp.bfloat16)
    one = jnp.ones((), jnp.bfloat16)
    lane_group = iota((BOTH, LANES), 1) // LOW

    @pl.when((pl.program_id(0) == 0) & (pl.program_id(1) == 0))
    def _():
        for c in range(chunks):
            for half in range(CHUNK // LANES):
                for s in range(2):
                    row = stats_ref[2 * c + half, s : s + 1, :].astype(jnp.bfloat16)
                    spread_ref[c, HIGH * s : HIGH * (s + 1), half * LANES : (half + 1) * LANES] = jnp.broadcast_to(
                        row, (HIGH, LANES)
                    )

    sums_ref[...] = jnp.zeros_like(sums_ref)
    for c in range(chunks):
        raw = jnp.concatenate([packed_ref[2 * c], packed_ref[2 * c + 1]], axis=1)
        grad = spread_ref[c, 0:HIGH]
        hess = spread_ref[c, HIGH:BOTH]
        n = table_ref[3 * NODES, c]
        for q in range(per_step):
            words = raw >> ((pl.program_id(1) * per_step + q) * 8)
            low = (words & (LOW - 1)).astype(jnp.bfloat16)
            high = ((words >> 4) & (HIGH - 1)).astype(jnp.bfloat16)
            left = []
            right = []
            for j in range(8):
                hit = jnp.broadcast_to(high[j : j + 1], (HIGH, CHUNK)) == level
                left.append(jnp.where(hit, grad, zero))
                left.append(jnp.where(hit, hess, zero))
                right.append(jnp.where(jnp.broadcast_to(low[j : j + 1], (LOW, CHUNK)) == level, one, zero))
            product = dot_t(jnp.concatenate(left, 0), jnp.concatenate(right, 0))
            own = product[0:BOTH]
            for j in range(1, 8):
                own = jnp.where(lane_group == j, product[BOTH * j : BOTH * (j + 1)], own)
            sums_ref[q, n] = sums_ref[q, n] + own
    half = LANES // 2
    for q in range(per_step):
        for pair in range(NODES // 2):
            even = sums_ref[q, 2 * pair]
            odd = sums_ref[q, 2 * pair + 1]
            first = jnp.concatenate([even[:, :half], odd[:, :half]], axis=1)
            second = jnp.concatenate([even[:, half:], odd[:, half:]], axis=1)
            keep_ref[q, 0, pair] = jnp.where(core == 0, first, second)
            send_ref[q, 0, pair] = jnp.where(core == 0, second, first)


def histogram(core, table, packed, stats, rows, per_step=4):
    room, words, _ = packed.shape
    blocks = words // 8
    chunks = rows // CHUNK + NODES - 1
    out = jax.ShapeDtypeStruct((BYTES, blocks, NODES // 2, BOTH, LANES), jnp.float32)
    keep, send = pl.pallas_call(
        functools.partial(hist_kernel, chunks, per_step),
        grid=(blocks, BYTES // per_step),
        in_specs=[
            pl.BlockSpec(memory_space=pltpu.SMEM),
            pl.BlockSpec(memory_space=pltpu.SMEM),
            pl.BlockSpec((room, 8, LANES), lambda i, k: (0, i, 0)),
            pl.BlockSpec((room, 8, LANES), lambda i, k: (0, 0, 0)),
        ],
        out_specs=[pl.BlockSpec((per_step, 1, NODES // 2, BOTH, LANES), lambda i, k: (k, i, 0, 0, 0))] * 2,
        out_shape=[out, out],
        scratch_shapes=[
            pltpu.VMEM((chunks, BOTH, CHUNK), jnp.bfloat16),
            pltpu.VMEM((per_step, NODES, BOTH, LANES), jnp.float32),
        ],
        compiler_params=pltpu.CompilerParams(vmem_limit_bytes=32 * 2**20),
        name="histogram",
    )(core, table, packed, stats)
    return [v.reshape(BYTES * blocks, NODES // 2, BOTH, LANES) for v in (keep, send)]


def gain_kernel(parts_ref, gain_ref, best_ref):
    hist = parts_ref[0]
    for i in range(1, parts_ref.shape[0]):
        hist = hist + parts_ref[i]
    rows = hist.shape[0]
    row_a, row_b = iota((rows, rows), 0), iota((rows, rows), 1)
    lane_a, lane_b = iota((LANES, LANES), 0), iota((LANES, LANES), 1)
    same_lows = lane_a // LOW == lane_b // LOW
    same_highs = row_a // HIGH == row_b // HIGH
    within = exact_dot(hist, ones_where(same_lows & (lane_a <= lane_b)))
    summed = exact_dot(hist, ones_where(same_lows))
    left = within + exact_dot(ones_where(same_highs & (row_a > row_b)), summed)
    total = exact_dot(ones_where(same_highs), summed)
    left = left.reshape(NODES // 2, 2, HIGH, LANES)
    total = total.reshape(NODES // 2, 2, HIGH, LANES)
    grad_left, hess_left = left[:, 0], left[:, 1]
    grad_total, hess_total = total[:, 0], total[:, 1]
    gain = grad_left * grad_left / (hess_left + 1.0)
    gain = gain + (grad_total - grad_left) ** 2 / (hess_total - hess_left + 1.0)
    gain = gain - grad_total * grad_total / (hess_total + 1.0)
    most = jnp.max(gain, axis=1)
    half = LANES // 2
    for odd in range(2):
        best = jnp.max(most[:, odd * half : (odd + 1) * half], axis=1, keepdims=True)
        for pair in range(NODES // 2):
            best_ref[2 * pair + odd] = jnp.broadcast_to(best[pair], (LANES,))
    gain = gain.reshape(NODES // 2 * HIGH, LANES)
    from_lane, to_bin = iota((LANES, BINS), 0), iota((LANES, BINS), 1)
    own_high = iota((NODES // 2 * HIGH, BINS), 0) % HIGH == iota((NODES // 2 * HIGH, BINS), 1) // LOW
    for odd in range(2):
        for slot in range(SHARE):
            take = ones_where(from_lane == (odd * SHARE + slot) * LOW + to_bin % LOW)
            spread = jnp.where(own_high, exact_dot(gain, take), 0.0)
            rows_out = jnp.sum(spread.reshape(NODES // 2, HIGH, BINS), axis=1)
            for pair in range(NODES // 2):
                gain_ref[slot, 2 * pair + odd] = rows_out[pair]


def gains(parts):
    chips = parts.shape[0]
    return pl.pallas_call(
        gain_kernel,
        out_shape=(
            jax.ShapeDtypeStruct((SHARE, NODES, BINS), jnp.float32),
            jax.ShapeDtypeStruct((NODES, LANES), jnp.float32),
        ),
        compiler_params=pltpu.CompilerParams(vmem_limit_bytes=32 * 2**20),
        name="gains",
    )(parts.reshape(chips, NODES // 2 * BOTH, LANES))


def per_device(bins, grads, hess, node):
    row_size = lax.axis_size("row")
    feat_size = lax.axis_size("feat")
    swap = [(i, i ^ 1) for i in range(row_size)]
    same_core = [[chip * CORES + c for chip in range(row_size // CORES)] for c in range(CORES)]
    core = (lax.axis_index("row") % CORES)[None]
    table, order = plan(node)
    packed, stats = place(table, order, bins, grads, hess)
    keep, send = histogram(core, table, packed, stats, bins.shape[1])
    pair = keep + lax.ppermute(send, "row", swap)
    gain, own_best = gains(lax.all_to_all(pair, "row", 0, 0, axis_index_groups=same_core, tiled=True))
    copies = jnp.broadcast_to(own_best[:, 0], (row_size * feat_size, NODES))
    best = jnp.max(lax.all_to_all(copies, ("row", "feat"), 0, 0, tiled=True), axis=0)
    return (gain - best[None, :, None], best)


def solution(mesh):
    return jax.shard_map(
        per_device,
        mesh=mesh,
        in_specs=(P("feat", "row"), P("row"), P("row"), P("row")),
        out_specs=(P(("feat", "row"), None, None), P()),
        check_vma=False,
    )
```

```python
import functools

import jax
import jax.numpy as jnp
from jax import lax
from jax.experimental import pallas as pl
from jax.experimental.pallas import tpu as pltpu
from jax.sharding import PartitionSpec as P

BINS = 256
NODES = 8
LANES = 128
CHUNK = 256
LOW = 16
HIGH = BINS // LOW
CORES = 2
SHARE = 4
BYTES = 4
TILES = 16
OWNER = 3 * NODES
LIMIT = OWNER + 1
BOTH = 2 * HIGH


def iota(shape, dim):
    return lax.broadcasted_iota(jnp.int32, shape, dim)


def ones_where(condition, dtype=jnp.float32):
    return jnp.where(condition, 1.0, 0.0).astype(dtype)


def tiled(row):
    return pltpu.with_memory_space_constraint(row.reshape(row.shape[0] // LANES, LANES), pltpu.HBM)


def exact_dot(a, b):
    return jnp.dot(a, b, preferred_element_type=jnp.float32, precision=lax.Precision.HIGHEST)


def dot_t(a, b):
    return lax.dot_general(a, b, (((1,), (1,)), ((), ())), preferred_element_type=jnp.float32)


def three(x):
    first = x.astype(jnp.bfloat16)
    rest = x - first.astype(jnp.float32)
    second = rest.astype(jnp.bfloat16)
    return [first, second, (rest - second.astype(jnp.float32)).astype(jnp.bfloat16)]


def times_ones(x, ones):
    rows = x.shape[0]
    parts = jnp.dot(jnp.concatenate(three(x), 0), ones, preferred_element_type=jnp.float32)
    return parts[:rows] + parts[rows : 2 * rows] + parts[2 * rows :]


def ones_times(ones, x):
    lanes = x.shape[1]
    parts = jnp.dot(ones, jnp.concatenate(three(x), 1), preferred_element_type=jnp.float32)
    return parts[:, :lanes] + parts[:, lanes : 2 * lanes] + parts[:, 2 * lanes :]


def write_plan(node_ref, table_ref, order_ref):
    tiles = node_ref.shape[0]
    node = node_ref[...]
    members = [node == n for n in range(NODES)]
    stacked = jnp.concatenate([ones_where(m) for m in members], 0).astype(jnp.bfloat16)
    before = ones_where(iota((LANES, LANES), 0) < iota((LANES, LANES), 1), jnp.bfloat16)
    ranks = jnp.dot(stacked, before, preferred_element_type=jnp.float32)
    place = jnp.zeros((tiles, LANES), jnp.float32)
    first = jnp.zeros((tiles, 1), jnp.float32)
    counts = jnp.zeros((NODES, tiles), jnp.float32)
    for n in range(NODES):
        at = slice(n * tiles, (n + 1) * tiles)
        place = place + jnp.where(members[n], ranks[at] + first, 0.0)
        first = first + jnp.sum(ones_where(members[n]), axis=1, keepdims=True)
        counts = counts + dot_t(ones_where(iota((NODES, LANES), 0) == n, jnp.bfloat16), stacked[at])
    earlier = exact_dot(counts, ones_where(iota((tiles, tiles), 0) < iota((tiles, tiles), 1)))
    lower = ones_where(iota((NODES, NODES), 0) > iota((NODES, NODES), 1))
    start = exact_dot(lower, counts)
    total = jnp.sum(counts, axis=1, keepdims=True).astype(jnp.int32)
    padded = ((total + (CHUNK - 1)) // CHUNK * CHUNK).astype(jnp.float32)
    base = exact_dot(lower, jnp.broadcast_to(padded, (NODES, LANES)))
    at_chunk = (iota((NODES, LANES), 1) * CHUNK).astype(jnp.float32)
    holds = ones_where((base <= at_chunk) & (at_chunk < base + padded))
    owner = jnp.sum(holds * iota((NODES, LANES), 0).astype(jnp.float32), axis=0, keepdims=True)
    limit = jnp.sum(holds * (base + total.astype(jnp.float32)), axis=0, keepdims=True)
    table_ref[0:NODES, :tiles] = (base[:, :tiles] + earlier).astype(jnp.int32)
    table_ref[NODES : 2 * NODES, :tiles] = counts.astype(jnp.int32)
    table_ref[2 * NODES : 3 * NODES, :tiles] = start.astype(jnp.int32)
    table_ref[OWNER : OWNER + 1, :] = owner.astype(jnp.int32)
    table_ref[LIMIT : LIMIT + 1, :] = limit.astype(jnp.int32)
    lane = iota((8, LANES), 1).astype(jnp.bfloat16)
    slot = iota((LANES, LANES), 0).astype(jnp.float32)
    for t in range(tiles):
        hit = ones_where(jnp.broadcast_to(place[t : t + 1], (LANES, LANES)) == slot, jnp.bfloat16)
        order_ref[t] = dot_t(lane, hit).astype(jnp.int32)


def place_kernel(
    node_ref, bins_ref, grads_ref, hess_ref, packed_ref, stats_ref, plan_ref, order_ref, words_ref, pairs_ref, table_ref, done
):
    step = pl.program_id(0)

    @pl.when(step == 0)
    def _():
        plan_ref[...] = jnp.zeros_like(plan_ref)
        write_plan(node_ref, plan_ref, order_ref)

    lane = iota((8, LANES), 1)
    top = iota((8, LANES), 0) == 0
    groups = packed_ref.shape[1] // 8
    for i in range(TILES):
        at = slice(i * LANES, (i + 1) * LANES)
        t = step * TILES + i
        order = order_ref[t]
        for g in range(groups):
            word = bins_ref[8 * g : 8 * g + 8, at]
            for k in range(1, BYTES):
                first = 8 * (g + groups * k)
                word = word | (bins_ref[first : first + 8, at] << (8 * k))
            words_ref[t, 8 * g : 8 * g + 8] = jnp.take_along_axis(word, order, axis=1)
        grad = jnp.broadcast_to(grads_ref[i : i + 1].astype(jnp.float32), (8, LANES))
        hess = jnp.broadcast_to(hess_ref[i : i + 1].astype(jnp.float32), (8, LANES))
        pairs_ref[t] = jnp.take_along_axis(jnp.where(top, grad, hess), order, axis=1)

    @pl.when(step == pl.num_programs(0) - 1)
    def _():
        copy = pltpu.make_async_copy(plan_ref, table_ref, done)
        copy.start()
        copy.wait()

        def store(tile, values):
            for g in range(groups):
                packed_ref[tile, 8 * g : 8 * g + 8] = values[g]
            stats_ref[tile] = values[groups]

        tiles = words_ref.shape[0]
        for n in range(NODES):

            def append(t, state):
                _, held = state
                dest = table_ref[n, t]
                count = table_ref[NODES + n, t]
                start = table_ref[2 * NODES + n, t]
                off = dest & (LANES - 1)
                shift = (off - start) & (LANES - 1)
                full = jnp.broadcast_to(off + count, (8, LANES)) >= LANES
                filled = lane < off
                runs = [words_ref[t, 8 * g : 8 * g + 8] for g in range(groups)] + [pairs_ref[t]]
                runs = [pltpu.roll(run, shift, axis=1) for run in runs]
                now = [jnp.where(filled, old, run) for old, run in zip(held, runs)]
                store(dest >> 7, now)
                return dest + count, tuple(jnp.where(full, run, new) for run, new in zip(runs, now))

            empty = tuple(jnp.zeros((8, LANES), jnp.int32) for _ in range(groups)) + (jnp.zeros((8, LANES), jnp.float32),)
            last, held = lax.fori_loop(0, tiles, append, (jnp.int32(0), empty), unroll=64)
            store(last >> 7, held)


def place(bins, grads, hess, node):
    features, rows = bins.shape
    tiles = rows // LANES
    room = tiles + 2 * NODES
    words = features // BYTES
    table = (4 * NODES, LANES)
    packed, stats, plan = pl.pallas_call(
        place_kernel,
        grid=(tiles // TILES,),
        in_specs=[
            pl.BlockSpec((tiles, LANES), lambda i: (0, 0)),
            pl.BlockSpec((features, TILES * LANES), lambda i: (0, i)),
            pl.BlockSpec((TILES, LANES), lambda i: (i, 0)),
            pl.BlockSpec((TILES, LANES), lambda i: (i, 0)),
        ],
        out_specs=[
            pl.BlockSpec((room, words, LANES), lambda i: (0, 0, 0)),
            pl.BlockSpec((room, 8, LANES), lambda i: (0, 0, 0)),
            pl.BlockSpec(table, lambda i: (0, 0)),
        ],
        out_shape=[
            jax.ShapeDtypeStruct((room, words, LANES), jnp.int32),
            jax.ShapeDtypeStruct((room, 8, LANES), jnp.float32),
            jax.ShapeDtypeStruct(table, jnp.int32),
        ],
        scratch_shapes=[
            pltpu.VMEM((tiles, 8, LANES), jnp.int32),
            pltpu.VMEM((tiles, words, LANES), jnp.int32),
            pltpu.VMEM((tiles, 8, LANES), jnp.float32),
            pltpu.SMEM(table, jnp.int32),
            pltpu.SemaphoreType.DMA(()),
        ],
        compiler_params=pltpu.CompilerParams(vmem_limit_bytes=50 * 2**20),
        name="place",
    )(tiled(node), bins, tiled(grads), tiled(hess))
    return plan, packed, stats


def hist_kernel(chunks, per_step, core_ref, table_ref, packed_ref, stats_ref, keep_ref, send_ref, spread_ref, sums_ref):
    core = core_ref[0]
    level = iota((HIGH, CHUNK), 0).astype(jnp.bfloat16)
    zero = jnp.zeros((), jnp.bfloat16)
    one = jnp.ones((), jnp.bfloat16)
    lane_group = iota((BOTH, LANES), 1) // LOW

    @pl.when((pl.program_id(0) == 0) & (pl.program_id(1) == 0))
    def _():
        lane = iota((1, LANES), 1)
        for c in range(chunks):
            for half in range(CHUNK // LANES):
                valid = lane + (c * CHUNK + half * LANES) < table_ref[LIMIT, c]
                for s in range(2):
                    row = jnp.where(valid, stats_ref[2 * c + half, s : s + 1, :], 0.0).astype(jnp.bfloat16)
                    spread_ref[c, HIGH * s : HIGH * (s + 1), half * LANES : (half + 1) * LANES] = jnp.broadcast_to(
                        row, (HIGH, LANES)
                    )

    sums_ref[...] = jnp.zeros_like(sums_ref)
    for c in range(chunks):
        raw = jnp.concatenate([packed_ref[2 * c], packed_ref[2 * c + 1]], axis=1)
        grad = spread_ref[c, 0:HIGH]
        hess = spread_ref[c, HIGH:BOTH]
        n = table_ref[OWNER, c]
        for q in range(per_step):
            words = raw >> ((pl.program_id(1) * per_step + q) * 8)
            low = (words & (LOW - 1)).astype(jnp.bfloat16)
            high = ((words >> 4) & (HIGH - 1)).astype(jnp.bfloat16)
            left = []
            right = []
            for j in range(8):
                hit = jnp.broadcast_to(high[j : j + 1], (HIGH, CHUNK)) == level
                left.append(jnp.where(hit, grad, zero))
                left.append(jnp.where(hit, hess, zero))
                right.append(jnp.where(jnp.broadcast_to(low[j : j + 1], (LOW, CHUNK)) == level, one, zero))
            product = dot_t(jnp.concatenate(left, 0), jnp.concatenate(right, 0))
            own = product[0:BOTH]
            for j in range(1, 8):
                own = jnp.where(lane_group == j, product[BOTH * j : BOTH * (j + 1)], own)
            sums_ref[q, n] = sums_ref[q, n] + own
    half = LANES // 2
    for q in range(per_step):
        for pair in range(NODES // 2):
            even = sums_ref[q, 2 * pair]
            odd = sums_ref[q, 2 * pair + 1]
            first = jnp.concatenate([even[:, :half], odd[:, :half]], axis=1)
            second = jnp.concatenate([even[:, half:], odd[:, half:]], axis=1)
            keep_ref[q, 0, pair] = jnp.where(core == 0, first, second)
            send_ref[q, 0, pair] = jnp.where(core == 0, second, first)


def histogram(core, table, packed, stats, rows, per_step=4):
    room, words, _ = packed.shape
    blocks = words // 8
    chunks = rows // CHUNK + NODES - 1
    out = jax.ShapeDtypeStruct((BYTES, blocks, NODES // 2, BOTH, LANES), jnp.float32)
    keep, send = pl.pallas_call(
        functools.partial(hist_kernel, chunks, per_step),
        grid=(blocks, BYTES // per_step),
        in_specs=[
            pl.BlockSpec(memory_space=pltpu.SMEM),
            pl.BlockSpec(memory_space=pltpu.SMEM),
            pl.BlockSpec((room, 8, LANES), lambda i, k: (0, i, 0)),
            pl.BlockSpec((room, 8, LANES), lambda i, k: (0, 0, 0)),
        ],
        out_specs=[pl.BlockSpec((per_step, 1, NODES // 2, BOTH, LANES), lambda i, k: (k, i, 0, 0, 0))] * 2,
        out_shape=[out, out],
        scratch_shapes=[
            pltpu.VMEM((chunks, BOTH, CHUNK), jnp.bfloat16),
            pltpu.VMEM((per_step, NODES, BOTH, LANES), jnp.float32),
        ],
        compiler_params=pltpu.CompilerParams(vmem_limit_bytes=32 * 2**20),
        name="histogram",
    )(core, table, packed, stats)
    return [v.reshape(BYTES * blocks, NODES // 2, BOTH, LANES) for v in (keep, send)]


def gain_kernel(parts_ref, gain_ref, best_ref):
    hist = parts_ref[0]
    for i in range(1, parts_ref.shape[0]):
        hist = hist + parts_ref[i]
    rows = hist.shape[0]
    row_a, row_b = iota((rows, rows), 0), iota((rows, rows), 1)
    lane_a, lane_b = iota((LANES, LANES), 0), iota((LANES, LANES), 1)
    same_lows = lane_a // LOW == lane_b // LOW
    same_highs = row_a // HIGH == row_b // HIGH
    bf16 = jnp.bfloat16
    both = jnp.concatenate([ones_where(same_lows & (lane_a <= lane_b), bf16), ones_where(same_lows, bf16)], 1)
    within = times_ones(hist, both)
    within, summed = within[:, :LANES], within[:, LANES:]
    both = jnp.concatenate([ones_where(same_highs & (row_a > row_b), bf16), ones_where(same_highs, bf16)], 0)
    above = ones_times(both, summed)
    left = within + above[:rows]
    total = above[rows:]
    left = left.reshape(NODES // 2, 2, HIGH, LANES)
    total = total.reshape(NODES // 2, 2, HIGH, LANES)
    grad_left, hess_left = left[:, 0], left[:, 1]
    grad_total, hess_total = total[:, 0], total[:, 1]
    gain = grad_left * grad_left / (hess_left + 1.0)
    gain = gain + (grad_total - grad_left) ** 2 / (hess_total - hess_left + 1.0)
    gain = gain - grad_total * grad_total / (hess_total + 1.0)
    most = jnp.max(gain, axis=1)
    half = LANES // 2
    for odd in range(2):
        best = jnp.max(most[:, odd * half : (odd + 1) * half], axis=1, keepdims=True)
        for pair in range(NODES // 2):
            best_ref[2 * pair + odd] = jnp.broadcast_to(best[pair], (LANES,))
    gain = gain.reshape(NODES // 2 * HIGH, LANES)
    from_lane, to_bin = iota((LANES, BINS), 0), iota((LANES, BINS), 1)
    own_high = iota((NODES // 2 * HIGH, BINS), 0) % HIGH == iota((NODES // 2 * HIGH, BINS), 1) // LOW
    for odd in range(2):
        for slot in range(SHARE):
            take = ones_where(from_lane == (odd * SHARE + slot) * LOW + to_bin % LOW, bf16)
            spread = jnp.where(own_high, times_ones(gain, take), 0.0)
            rows_out = jnp.sum(spread.reshape(NODES // 2, HIGH, BINS), axis=1)
            for pair in range(NODES // 2):
                gain_ref[slot, 2 * pair + odd] = rows_out[pair]


def gains(parts):
    chips = parts.shape[0]
    return pl.pallas_call(
        gain_kernel,
        out_shape=(
            jax.ShapeDtypeStruct((SHARE, NODES, BINS), jnp.float32),
            jax.ShapeDtypeStruct((NODES, LANES), jnp.float32),
        ),
        compiler_params=pltpu.CompilerParams(vmem_limit_bytes=32 * 2**20),
        name="gains",
    )(parts.reshape(chips, NODES // 2 * BOTH, LANES))


def per_device(bins, grads, hess, node):
    row_size = lax.axis_size("row")
    feat_size = lax.axis_size("feat")
    swap = [(i, i ^ 1) for i in range(row_size)]
    same_core = [[chip * CORES + c for chip in range(row_size // CORES)] for c in range(CORES)]
    core = (lax.axis_index("row") % CORES)[None]
    table, packed, stats = place(bins, grads, hess, node)
    keep, send = histogram(core, table, packed, stats, bins.shape[1])
    pair = keep + lax.ppermute(send, "row", swap)
    gain, own_best = gains(lax.all_to_all(pair, "row", 0, 0, axis_index_groups=same_core, tiled=True))
    copies = jnp.broadcast_to(own_best[:, 0], (row_size * feat_size, NODES))
    best = jnp.max(lax.all_to_all(copies, ("row", "feat"), 0, 0, tiled=True), axis=0)
    return (gain - best[None, :, None], best)


def solution(mesh):
    return jax.shard_map(
        per_device,
        mesh=mesh,
        in_specs=(P("feat", "row"), P("row"), P("row"), P("row")),
        out_specs=(P(("feat", "row"), None, None), P()),
        check_vma=False,
    )
```

```python
import functools

import jax
import jax.numpy as jnp
from jax import lax
from jax.experimental import pallas as pl
from jax.experimental.pallas import tpu as pltpu
from jax.sharding import PartitionSpec as P

BINS = 256
NODES = 8
LANES = 128
CHUNK = 256
LOW = 16
HIGH = BINS // LOW
CORES = 2
SHARE = 4
BYTES = 4
TILES = 64
OWNER = 3 * NODES
LIMIT = OWNER + 1
BOTH = 2 * HIGH


def iota(shape, dim):
    return lax.broadcasted_iota(jnp.int32, shape, dim)


def ones_where(condition, dtype=jnp.float32):
    return jnp.where(condition, 1.0, 0.0).astype(dtype)


def tiled(row):
    return pltpu.with_memory_space_constraint(row.reshape(row.shape[0] // LANES, LANES), pltpu.HBM)


def exact_dot(a, b):
    return jnp.dot(a, b, preferred_element_type=jnp.float32, precision=lax.Precision.HIGHEST)


def dot_t(a, b):
    return lax.dot_general(a, b, (((1,), (1,)), ((), ())), preferred_element_type=jnp.float32)


def three(x):
    first = x.astype(jnp.bfloat16)
    rest = x - first.astype(jnp.float32)
    second = rest.astype(jnp.bfloat16)
    return [first, second, (rest - second.astype(jnp.float32)).astype(jnp.bfloat16)]


def times_ones(x, ones):
    rows = x.shape[0]
    parts = jnp.dot(jnp.concatenate(three(x), 0), ones, preferred_element_type=jnp.float32)
    return parts[:rows] + parts[rows : 2 * rows] + parts[2 * rows :]


def ones_times(ones, x):
    lanes = x.shape[1]
    parts = jnp.dot(ones, jnp.concatenate(three(x), 1), preferred_element_type=jnp.float32)
    return parts[:, :lanes] + parts[:, lanes : 2 * lanes] + parts[:, 2 * lanes :]


def write_plan(node_ref, table_ref, order_ref):
    tiles = node_ref.shape[0]
    node = node_ref[...]
    members = [node == n for n in range(NODES)]
    stacked = jnp.concatenate([ones_where(m) for m in members], 0).astype(jnp.bfloat16)
    before = ones_where(iota((LANES, LANES), 0) < iota((LANES, LANES), 1), jnp.bfloat16)
    ranks = jnp.dot(stacked, before, preferred_element_type=jnp.float32)
    place = jnp.zeros((tiles, LANES), jnp.float32)
    first = jnp.zeros((tiles, 1), jnp.float32)
    counts = jnp.zeros((NODES, tiles), jnp.float32)
    for n in range(NODES):
        at = slice(n * tiles, (n + 1) * tiles)
        place = place + jnp.where(members[n], ranks[at] + first, 0.0)
        first = first + jnp.sum(ones_where(members[n]), axis=1, keepdims=True)
        counts = counts + dot_t(ones_where(iota((NODES, LANES), 0) == n, jnp.bfloat16), stacked[at])
    earlier = exact_dot(counts, ones_where(iota((tiles, tiles), 0) < iota((tiles, tiles), 1)))
    lower = ones_where(iota((NODES, NODES), 0) > iota((NODES, NODES), 1))
    start = exact_dot(lower, counts)
    total = jnp.sum(counts, axis=1, keepdims=True).astype(jnp.int32)
    padded = ((total + (CHUNK - 1)) // CHUNK * CHUNK).astype(jnp.float32)
    base = exact_dot(lower, jnp.broadcast_to(padded, (NODES, LANES)))
    at_chunk = (iota((NODES, LANES), 1) * CHUNK).astype(jnp.float32)
    holds = ones_where((base <= at_chunk) & (at_chunk < base + padded))
    owner = jnp.sum(holds * iota((NODES, LANES), 0).astype(jnp.float32), axis=0, keepdims=True)
    limit = jnp.sum(holds * (base + total.astype(jnp.float32)), axis=0, keepdims=True)
    table_ref[0:NODES, :tiles] = (base[:, :tiles] + earlier).astype(jnp.int32)
    table_ref[NODES : 2 * NODES, :tiles] = counts.astype(jnp.int32)
    table_ref[2 * NODES : 3 * NODES, :tiles] = start.astype(jnp.int32)
    table_ref[OWNER : OWNER + 1, :] = owner.astype(jnp.int32)
    table_ref[LIMIT : LIMIT + 1, :] = limit.astype(jnp.int32)
    lane = iota((8, LANES), 1).astype(jnp.bfloat16)
    slot = iota((LANES, LANES), 0).astype(jnp.float32)
    for t in range(tiles):
        hit = ones_where(jnp.broadcast_to(place[t : t + 1], (LANES, LANES)) == slot, jnp.bfloat16)
        order_ref[t] = dot_t(lane, hit).astype(jnp.int32)


def place_kernel(
    node_ref, bins_ref, grads_ref, hess_ref, packed_ref, stats_ref, plan_ref, order_ref, words_ref, pairs_ref, table_ref, done
):
    step = pl.program_id(0)

    @pl.when(step == 0)
    def _():
        plan_ref[...] = jnp.zeros_like(plan_ref)
        write_plan(node_ref, plan_ref, order_ref)

    lane = iota((8, LANES), 1)
    top = iota((8, LANES), 0) == 0
    groups = packed_ref.shape[1] // 8
    for i in range(TILES):
        at = slice(i * LANES, (i + 1) * LANES)
        t = step * TILES + i
        order = order_ref[t]
        for g in range(groups):
            word = bins_ref[8 * g : 8 * g + 8, at]
            for k in range(1, BYTES):
                first = 8 * (g + groups * k)
                word = word | (bins_ref[first : first + 8, at] << (8 * k))
            words_ref[t, 8 * g : 8 * g + 8] = jnp.take_along_axis(word, order, axis=1)
        grad = jnp.broadcast_to(grads_ref[i : i + 1].astype(jnp.float32), (8, LANES))
        hess = jnp.broadcast_to(hess_ref[i : i + 1].astype(jnp.float32), (8, LANES))
        pairs_ref[t] = jnp.take_along_axis(jnp.where(top, grad, hess), order, axis=1)

    @pl.when(step == pl.num_programs(0) - 1)
    def _():
        copy = pltpu.make_async_copy(plan_ref, table_ref, done)
        copy.start()
        copy.wait()

        def store(tile, values):
            for g in range(groups):
                packed_ref[tile, 8 * g : 8 * g + 8] = values[g]
            stats_ref[tile] = values[groups]

        tiles = words_ref.shape[0]
        for n in range(NODES):

            def append(t, state):
                _, held = state
                dest = table_ref[n, t]
                count = table_ref[NODES + n, t]
                start = table_ref[2 * NODES + n, t]
                off = dest & (LANES - 1)
                shift = (off - start) & (LANES - 1)
                full = jnp.broadcast_to(off + count, (8, LANES)) >= LANES
                filled = lane < off
                runs = [words_ref[t, 8 * g : 8 * g + 8] for g in range(groups)] + [pairs_ref[t]]
                runs = [pltpu.roll(run, shift, axis=1) for run in runs]
                now = [jnp.where(filled, old, run) for old, run in zip(held, runs)]
                store(dest >> 7, now)
                return dest + count, tuple(jnp.where(full, run, new) for run, new in zip(runs, now))

            empty = tuple(jnp.zeros((8, LANES), jnp.int32) for _ in range(groups)) + (jnp.zeros((8, LANES), jnp.float32),)
            last, held = lax.fori_loop(0, tiles, append, (jnp.int32(0), empty), unroll=64)
            store(last >> 7, held)


def place(bins, grads, hess, node):
    features, rows = bins.shape
    tiles = rows // LANES
    room = tiles + 2 * NODES
    words = features // BYTES
    table = (4 * NODES, LANES)
    packed, stats, plan = pl.pallas_call(
        place_kernel,
        grid=(tiles // TILES,),
        in_specs=[
            pl.BlockSpec((tiles, LANES), lambda i: (0, 0)),
            pl.BlockSpec((features, TILES * LANES), lambda i: (0, i)),
            pl.BlockSpec((TILES, LANES), lambda i: (i, 0)),
            pl.BlockSpec((TILES, LANES), lambda i: (i, 0)),
        ],
        out_specs=[
            pl.BlockSpec((room, words, LANES), lambda i: (0, 0, 0)),
            pl.BlockSpec((room, 8, LANES), lambda i: (0, 0, 0)),
            pl.BlockSpec(table, lambda i: (0, 0)),
        ],
        out_shape=[
            jax.ShapeDtypeStruct((room, words, LANES), jnp.int32),
            jax.ShapeDtypeStruct((room, 8, LANES), jnp.float32),
            jax.ShapeDtypeStruct(table, jnp.int32),
        ],
        scratch_shapes=[
            pltpu.VMEM((tiles, 8, LANES), jnp.int32),
            pltpu.VMEM((tiles, words, LANES), jnp.int32),
            pltpu.VMEM((tiles, 8, LANES), jnp.float32),
            pltpu.SMEM(table, jnp.int32),
            pltpu.SemaphoreType.DMA(()),
        ],
        compiler_params=pltpu.CompilerParams(vmem_limit_bytes=50 * 2**20),
        name="place",
    )(tiled(node), bins, tiled(grads), tiled(hess))
    return plan, packed, stats


def hist_kernel(chunks, per_step, core_ref, table_ref, packed_ref, stats_ref, keep_ref, send_ref, spread_ref, sums_ref):
    core = core_ref[0]
    level = iota((HIGH, CHUNK), 0).astype(jnp.bfloat16)
    zero = jnp.zeros((), jnp.bfloat16)
    one = jnp.ones((), jnp.bfloat16)
    lane_group = iota((BOTH, LANES), 1) // LOW

    @pl.when((pl.program_id(0) == 0) & (pl.program_id(1) == 0))
    def _():
        lane = iota((1, LANES), 1)
        for c in range(chunks):
            for half in range(CHUNK // LANES):
                valid = lane + (c * CHUNK + half * LANES) < table_ref[LIMIT, c]
                for s in range(2):
                    row = jnp.where(valid, stats_ref[2 * c + half, s : s + 1, :], 0.0).astype(jnp.bfloat16)
                    spread_ref[c, HIGH * s : HIGH * (s + 1), half * LANES : (half + 1) * LANES] = jnp.broadcast_to(
                        row, (HIGH, LANES)
                    )

    sums_ref[...] = jnp.zeros_like(sums_ref)
    for c in range(chunks):
        raw = jnp.concatenate([packed_ref[2 * c], packed_ref[2 * c + 1]], axis=1)
        grad = spread_ref[c, 0:HIGH]
        hess = spread_ref[c, HIGH:BOTH]
        n = table_ref[OWNER, c]
        for q in range(per_step):
            words = raw >> ((pl.program_id(1) * per_step + q) * 8)
            low = (words & (LOW - 1)).astype(jnp.bfloat16)
            high = ((words >> 4) & (HIGH - 1)).astype(jnp.bfloat16)
            left = []
            right = []
            for j in range(8):
                hit = jnp.broadcast_to(high[j : j + 1], (HIGH, CHUNK)) == level
                left.append(jnp.where(hit, grad, zero))
                left.append(jnp.where(hit, hess, zero))
                right.append(jnp.where(jnp.broadcast_to(low[j : j + 1], (LOW, CHUNK)) == level, one, zero))
            product = dot_t(jnp.concatenate(left, 0), jnp.concatenate(right, 0))
            own = product[0:BOTH]
            for j in range(1, 8):
                own = jnp.where(lane_group == j, product[BOTH * j : BOTH * (j + 1)], own)
            sums_ref[q, n] = sums_ref[q, n] + own
    half = LANES // 2
    for q in range(per_step):
        for pair in range(NODES // 2):
            even = sums_ref[q, 2 * pair]
            odd = sums_ref[q, 2 * pair + 1]
            first = jnp.concatenate([even[:, :half], odd[:, :half]], axis=1)
            second = jnp.concatenate([even[:, half:], odd[:, half:]], axis=1)
            keep_ref[q, 0, pair] = jnp.where(core == 0, first, second)
            send_ref[q, 0, pair] = jnp.where(core == 0, second, first)


def histogram(core, table, packed, stats, rows, per_step=4):
    room, words, _ = packed.shape
    blocks = words // 8
    chunks = rows // CHUNK + NODES - 1
    out = jax.ShapeDtypeStruct((BYTES, blocks, NODES // 2, BOTH, LANES), jnp.float32)
    keep, send = pl.pallas_call(
        functools.partial(hist_kernel, chunks, per_step),
        grid=(blocks, BYTES // per_step),
        in_specs=[
            pl.BlockSpec(memory_space=pltpu.SMEM),
            pl.BlockSpec(memory_space=pltpu.SMEM),
            pl.BlockSpec((room, 8, LANES), lambda i, k: (0, i, 0)),
            pl.BlockSpec((room, 8, LANES), lambda i, k: (0, 0, 0)),
        ],
        out_specs=[pl.BlockSpec((per_step, 1, NODES // 2, BOTH, LANES), lambda i, k: (k, i, 0, 0, 0))] * 2,
        out_shape=[out, out],
        scratch_shapes=[
            pltpu.VMEM((chunks, BOTH, CHUNK), jnp.bfloat16),
            pltpu.VMEM((per_step, NODES, BOTH, LANES), jnp.float32),
        ],
        compiler_params=pltpu.CompilerParams(vmem_limit_bytes=32 * 2**20),
        name="histogram",
    )(core, table, packed, stats)
    return [v.reshape(BYTES * blocks, NODES // 2, BOTH, LANES) for v in (keep, send)]


def gain_kernel(parts_ref, gain_ref, best_ref):
    hist = parts_ref[0]
    for i in range(1, parts_ref.shape[0]):
        hist = hist + parts_ref[i]
    rows = hist.shape[0]
    row_a, row_b = iota((rows, rows), 0), iota((rows, rows), 1)
    lane_a, lane_b = iota((LANES, LANES), 0), iota((LANES, LANES), 1)
    same_lows = lane_a // LOW == lane_b // LOW
    same_highs = row_a // HIGH == row_b // HIGH
    bf16 = jnp.bfloat16
    both = jnp.concatenate([ones_where(same_lows & (lane_a <= lane_b), bf16), ones_where(same_lows, bf16)], 1)
    within = times_ones(hist, both)
    within, summed = within[:, :LANES], within[:, LANES:]
    both = jnp.concatenate([ones_where(same_highs & (row_a > row_b), bf16), ones_where(same_highs, bf16)], 0)
    above = ones_times(both, summed)
    left = within + above[:rows]
    total = above[rows:]
    left = left.reshape(NODES // 2, 2, HIGH, LANES)
    total = total.reshape(NODES // 2, 2, HIGH, LANES)
    grad_left, hess_left = left[:, 0], left[:, 1]
    grad_total, hess_total = total[:, 0], total[:, 1]
    gain = grad_left * grad_left / (hess_left + 1.0)
    gain = gain + (grad_total - grad_left) ** 2 / (hess_total - hess_left + 1.0)
    gain = gain - grad_total * grad_total / (hess_total + 1.0)
    most = jnp.max(gain, axis=1)
    half = LANES // 2
    for odd in range(2):
        best = jnp.max(most[:, odd * half : (odd + 1) * half], axis=1, keepdims=True)
        for pair in range(NODES // 2):
            best_ref[2 * pair + odd] = jnp.broadcast_to(best[pair], (LANES,))
    gain = gain.reshape(NODES // 2 * HIGH, LANES)
    from_lane, to_bin = iota((LANES, BINS), 0), iota((LANES, BINS), 1)
    own_high = iota((NODES // 2 * HIGH, BINS), 0) % HIGH == iota((NODES // 2 * HIGH, BINS), 1) // LOW
    for odd in range(2):
        for slot in range(SHARE):
            take = ones_where(from_lane == (odd * SHARE + slot) * LOW + to_bin % LOW, bf16)
            spread = jnp.where(own_high, times_ones(gain, take), 0.0)
            rows_out = jnp.sum(spread.reshape(NODES // 2, HIGH, BINS), axis=1)
            for pair in range(NODES // 2):
                gain_ref[slot, 2 * pair + odd] = rows_out[pair]


def gains(parts):
    chips = parts.shape[0]
    return pl.pallas_call(
        gain_kernel,
        out_shape=(
            jax.ShapeDtypeStruct((SHARE, NODES, BINS), jnp.float32),
            jax.ShapeDtypeStruct((NODES, LANES), jnp.float32),
        ),
        compiler_params=pltpu.CompilerParams(vmem_limit_bytes=32 * 2**20),
        name="gains",
    )(parts.reshape(chips, NODES // 2 * BOTH, LANES))


def per_device(bins, grads, hess, node):
    row_size = lax.axis_size("row")
    feat_size = lax.axis_size("feat")
    swap = [(i, i ^ 1) for i in range(row_size)]
    same_core = [[chip * CORES + c for chip in range(row_size // CORES)] for c in range(CORES)]
    core = (lax.axis_index("row") % CORES)[None]
    table, packed, stats = place(bins, grads, hess, node)
    keep, send = histogram(core, table, packed, stats, bins.shape[1])
    pair = keep + lax.ppermute(send, "row", swap)
    gain, own_best = gains(lax.all_to_all(pair, "row", 0, 0, axis_index_groups=same_core, tiled=True))
    copies = jnp.broadcast_to(own_best[:, 0], (row_size * feat_size, NODES))
    best = jnp.max(lax.all_to_all(copies, ("row", "feat"), 0, 0, tiled=True), axis=0)
    return (gain - best[None, :, None], best)


def solution(mesh):
    return jax.shard_map(
        per_device,
        mesh=mesh,
        in_specs=(P("feat", "row"), P("row"), P("row"), P("row")),
        out_specs=(P(("feat", "row"), None, None), P()),
        check_vma=False,
    )
```
